128 devices in a mesh: trip: 32 (over y, z, core), row: 4 (over x).
Axes of the slice: x: 4, y: 4, z: 4, core: 2. Of those that a mesh axis runs over, the one named last changes fastest.
Arguments:
- eigvecs: bfloat16 [8192, 64, 128], P(('trip', 'row')), may hold values from -0.5 to 0.5
- cubic: bfloat16 [3072, 64, 4096], P(('trip', 'row')), may hold values from -0.09375 to 0.09375
- triplets: int32 [3072, 3], P(('trip', 'row')), may hold values from 0 to 8191, as said below
- weights: int32 [3072], P(('trip', 'row')), may hold values from 1 to 6
- deviation: float32 [8192, 768], P(('trip', 'row')), may hold values from -6 to 6
- source: float32 [8192, 768], P(('trip', 'row')), may hold values from -6 to 6
- base_rate: float32 [8192, 64], P(('trip', 'row')), may hold values from 0.5 to 2
Outputs:
- relaxed: float32 [8192, 768], P(('trip', 'row'))
The draws below stay inside these ranges and needn't reach their ends.
Inputs may be any that keep to these rules, and one draw needn't show every extreme that they name: Column 0 of a device's triplets names wavevectors homed on devices of its own trip group; at most 12 of them on any one device, and in every trip group one device is named exactly 12 times by each device of the group. Columns 1 and 2 of one device's triplets together name at most 1 wavevectors homed on any one device, and one device is named exactly 1 times by every device. Wavevectors may repeat.
All inputs are finite; a program needn't handle non-finite values.
Results may differ from the reference program's by a relative error of at most 0.0003.
Values may be sent and summed in bfloat16 or wider, within the bound.
A program may use at most 128 MiB of HBM per device.

```python
import math
import jax
import jax.numpy as jnp
from jax import lax

NB = 64
COLS = 12
Q_DEV = 64
TRIP_DEV = 24
ITERS = 2
NQ = 8192
TRIPLET_TOTAL = 3072
CAP0 = 12
N_TRIP = 32
N_ROW = 4


def draw_triplets(key, part):
    devices = N_TRIP * N_ROW
    full_owner = jax.random.randint(jax.random.fold_in(key, 11), (), 0, devices)
    heavy_rows = jax.random.randint(jax.random.fold_in(key, 12), (N_TRIP,), 0, N_ROW)

    def one_device(device):
        sub = jax.random.fold_in(jax.random.fold_in(key, 13), device)
        keys = jax.random.split(sub, 7)
        group_id = device // N_ROW
        heavy_row = heavy_rows[group_id]
        offsets = jax.random.randint(keys[0], (TRIP_DEV,), 1, N_ROW)
        position = jnp.arange(TRIP_DEV)
        target = jnp.where(position < CAP0, heavy_row, (heavy_row + offsets) % N_ROW)
        first = (group_id * N_ROW + target) * Q_DEV + jax.random.randint(keys[1], (TRIP_DEV,), 0, Q_DEV)
        first = first[jax.random.permutation(keys[2], TRIP_DEV)]
        visit_order = jax.random.permutation(keys[3], devices)
        where_full = jnp.argmax(visit_order == full_owner)
        leading = visit_order[0]
        visit_order = visit_order.at[where_full].set(leading).at[0].set(full_owner)
        request = jnp.arange(2 * TRIP_DEV)
        owner_dev = visit_order[request % devices]
        second = owner_dev * Q_DEV + jax.random.randint(keys[5], (2 * TRIP_DEV,), 0, Q_DEV)
        second = second[jax.random.permutation(keys[6], 2 * TRIP_DEV)].reshape(TRIP_DEV, 2)
        return jnp.concatenate([first[:, None], second], axis=1)
    listed = jax.vmap(one_device)(jnp.arange(devices))
    return listed.reshape(TRIP_DEV * devices, 3).astype(jnp.int32)


def touch_ends(result, key, low, high):
    place = [jax.random.randint(jax.random.fold_in(key, axis), (), 0, length) for axis, length in enumerate(result.shape)]
    main_axis = result.shape.index(max(result.shape))
    next_to = place[:main_axis] + [(place[main_axis] + 1) % result.shape[main_axis]] + place[main_axis + 1:]
    return result.at[tuple(place)].set(low).at[tuple(next_to)].set(high)


def shard_levels(rng, extent, cuts, low, high):
    factor_of = 1.0
    for dim, parts in cuts:
        draws = jax.random.uniform(jax.random.fold_in(jax.random.fold_in(rng, 6), dim), (parts,), jnp.float32, low / len(cuts), high / len(cuts))
        factor_of = factor_of * jnp.repeat(jnp.exp(draws), extent[dim] // parts).reshape((-1,) + (1,) * (len(extent) - 1 - dim))
    return factor_of


def noise(own_key, shape, spread, most, shards=(), kind=jnp.bfloat16):
    drawn = jax.random.normal(own_key, shape, jnp.float32) * spread
    if len(shards) > 0:
        drawn = shard_levels(own_key, shape, shards, -0.22, 0.18) * drawn
    return jnp.clip(drawn, min=-most, max=most).astype(kind)


def setup_inputs(seed: int = 0) -> dict:
    streams_of = jax.random.split(jax.random.key(seed), 8)
    return {
        "eigvecs": noise(streams_of[0], (NQ, NB, 2 * NB), (2 * NB) ** -0.5, 0.5, ((0, 128),)),
        "cubic": noise(streams_of[1], (TRIPLET_TOTAL, NB, NB * NB), (NB * NB) ** -0.5, 0.09375, ((0, 128),)),
        "triplets": draw_triplets(jax.random.fold_in(streams_of[7], 71), 0),
        "weights": touch_ends(jax.random.randint(streams_of[3], (TRIPLET_TOTAL,), 1, 7), jax.random.fold_in(streams_of[3], 1), 1, 6).astype(jnp.int32),
        "deviation": noise(streams_of[4], (NQ, NB * COLS), 1.0, 6.0, ((0, 128),), jnp.float32),
        "source": noise(streams_of[5], (NQ, NB * COLS), 1.0, 6.0, ((0, 128),), jnp.float32),
        "base_rate": jnp.clip(jnp.exp(math.log(2.0) - 1.3862944 * jax.random.uniform(streams_of[6], (NQ, NB), jnp.float32) ** shard_levels(streams_of[6], (NQ, NB), ((0, 128),), -0.2, 0.2)), 0.5, 2.0),
    }


damping = 0.7


def contract(tensor, vec_one, vec_two, vec_three, weight):
    branches = vec_one.shape[0]
    flat = tensor.reshape(branches * branches, branches)
    section_one = jnp.dot(flat, vec_three, preferred_element_type=jnp.float32).astype(jnp.bfloat16)
    section_one = section_one.reshape(branches, branches, 2 * branches)
    section_two = jnp.einsum('ijx,jy->ixy', section_one.astype(jnp.float32), vec_two.astype(jnp.float32))
    real_part = section_two[:, :branches, :branches] - section_two[:, branches:, branches:]
    imag_part = section_two[:, :branches, branches:] + section_two[:, branches:, :branches]
    mixed = jnp.stack([real_part, imag_part], 1).astype(jnp.bfloat16).reshape(branches, 2 * branches * branches)
    section_three = jnp.dot(vec_one.T, mixed, preferred_element_type=jnp.float32)
    section_three = section_three.reshape(2, branches, 2, branches, branches)
    vreal = section_three[0, :, 0] - section_three[1, :, 1]
    vimag = section_three[0, :, 1] + section_three[1, :, 0]
    power = (vreal * vreal + vimag * vimag) * weight.astype(jnp.float32)
    return jnp.sum(power, 1).astype(jnp.bfloat16), jnp.sum(power, 2).astype(jnp.bfloat16)


def reference(eigvecs, cubic, triplets, weights, deviation, source, base_rate):
    def one_triplet(bundle):
        tensor, listed, weight = bundle
        chosen = jnp.take(eigvecs, listed, axis=0)
        return contract(tensor, chosen[0], chosen[1], chosen[2], weight)

    first_pairing, second_pairing = lax.map(one_triplet, (cubic, triplets, weights))
    row_index = triplets[:, 0]
    rate_terms = jnp.sum(first_pairing.astype(jnp.float32), 2) + jnp.sum(second_pairing.astype(jnp.float32), 2)
    total_rate = base_rate + jax.ops.segment_sum(rate_terms, row_index, num_segments=NQ)
    phonon_state = deviation.reshape(NQ, NB, COLS)
    driven = source.reshape(NQ, NB, COLS)
    for update in range(ITERS):
        coupling_factors = jnp.einsum('hzy,hye->hze', first_pairing.astype(jnp.float32), jnp.take(phonon_state, triplets[:, 1], axis=0), precision=lax.Precision.HIGHEST)
        coupling_factors = coupling_factors + jnp.einsum('hzy,hye->hze', second_pairing.astype(jnp.float32), jnp.take(phonon_state, triplets[:, 2], axis=0), precision=lax.Precision.HIGHEST)
        coupled = jax.ops.segment_sum(coupling_factors, row_index, num_segments=NQ)
        phonon_state = (1.0 - damping) * phonon_state + damping * (driven + coupled) / total_rate[:, :, None]
    return phonon_state.reshape(NQ, NB * COLS)
```

```python
import jax
import jax.numpy as jnp
from jax import lax
from jax.experimental import pallas as pl
from jax.experimental.pallas import tpu as pltpu
from jax.sharding import PartitionSpec as P

ITERS = 2
BRANCHES = 64


damping = 0.7


def ranks_of(target):
    chain_length = target.shape[0]
    matches = target[:, None] == target[None, :]
    earlier = lax.broadcasted_iota(
        jnp.int32, (chain_length, chain_length), 1
    ) < lax.broadcasted_iota(jnp.int32, (chain_length, chain_length), 0)
    return jnp.sum((matches & earlier).astype(jnp.int32), axis=1)


def slot_onehot(places, extent):
    return lax.broadcasted_iota(jnp.int32, (extent, places.shape[0]), 0) == places[None, :]


def pack_ints(places, values, extent):
    return jnp.sum(jnp.where(slot_onehot(places, extent), values[None, :], 0), axis=1)


def pack_rows(places, values, extent):
    onehot = slot_onehot(places, extent).astype(values.dtype)
    packed = jnp.dot(
        onehot, values, preferred_element_type=jnp.float32, precision=lax.Precision.HIGHEST
    )
    return packed.astype(values.dtype)


def contract_kernel(weight_ref, turned_ref, second_ref, third_ref, cubic_ref, picker_ref,
                    pair_one_ref, pair_two_ref, stacked, middle, spread, column_sums):
    half = BRANCHES
    wide = 2 * BRANCHES
    pairs = BRANCHES // 2
    lane = lax.broadcasted_iota(jnp.int32, (1, wide), 1)
    sign = jnp.where(lane < half, -1.0, 1.0)
    third = third_ref[0]
    swapped = (pltpu.roll(third.astype(jnp.float32), half, 1) * sign).astype(jnp.bfloat16)
    zero = jnp.zeros_like(third)
    mixer = jnp.concatenate(
        [
            jnp.concatenate([third, zero, swapped, zero], 0),
            jnp.concatenate([zero, third, zero, swapped], 0),
        ],
        1,
    )
    step = 1024
    for start in range(0, BRANCHES * BRANCHES, step):
        part = jnp.dot(
            turned_ref[0], cubic_ref[0, :, start : start + step],
            preferred_element_type=jnp.float32,
        ).astype(jnp.bfloat16)
        for offset in range(0, step, wide):
            row = (start + offset) // wide * half
            stacked[row : row + half, :wide] = part[:half, offset : offset + wide]
            stacked[row : row + half, wide:] = part[half:, offset : offset + wide]
    for start in range(0, pairs * half, 256):
        part = jnp.dot(
            stacked[start : start + 256, :], mixer, preferred_element_type=jnp.float32
        )
        middle[0, start : start + 256, :] = part[:, :wide]
        middle[1, start : start + 256, :] = part[:, wide:]
    group = 8
    total = jnp.zeros((half, wide), jnp.float32)
    for first in range(0, half, group):
        for a in range(first, first + group):
            place = (a % (2 * group)) * wide
            for side in range(2):
                value = middle[side, pl.ds(a, pairs, stride=half), :]
                turned = pltpu.roll(value, half, 1) * sign
                low = side * pairs
                spread[low : low + pairs, place : place + wide] = value.astype(jnp.bfloat16)
                spread[half + low : half + low + pairs, place : place + wide] = turned.astype(
                    jnp.bfloat16
                )
        begin = (first % (2 * group)) * wide
        found = jnp.dot(
            second_ref[0], spread[:, begin : begin + group * wide],
            preferred_element_type=jnp.float32,
        )
        square = found * found
        total = total + jnp.dot(
            square.astype(jnp.bfloat16),
            picker_ref[first * wide : (first + group) * wide, :],
            preferred_element_type=jnp.float32,
        )
        sums = jnp.sum(square, 0, keepdims=True)
        column_sums[first : first + group, :] = jnp.concatenate(
            [sums[:, q * wide : (q + 1) * wide] for q in range(group)], 0
        )
    weight = weight_ref[pl.program_id(0)].astype(jnp.float32)
    full = column_sums[...]
    full = (full + pltpu.roll(full, half, 1)) * weight
    pair_one_ref[0] = (total * weight).T[:half].astype(jnp.bfloat16)
    pair_two_ref[0] = full[:, :half].astype(jnp.bfloat16)


def contract_all(cubic, first_vecs, second_vecs, third_vecs, weights):
    count = cubic.shape[0]
    half = BRANCHES
    wide = 2 * half
    turned = jnp.swapaxes(first_vecs, 1, 2)
    second = second_vecs.reshape(count, half // 2, 2, 2, half)
    second = jnp.transpose(second, (0, 4, 3, 2, 1)).reshape(count, half, wide)
    picker = (
        lax.broadcasted_iota(jnp.int32, (half * wide, wide), 0) // wide
        == lax.broadcasted_iota(jnp.int32, (half * wide, wide), 1)
    ).astype(jnp.bfloat16)

    def block(*shape):
        return pl.BlockSpec((1,) + shape, lambda t: (t, 0, 0))

    pair = jax.ShapeDtypeStruct((count, half, half), jnp.bfloat16)
    return pl.pallas_call(
        contract_kernel,
        grid=(count,),
        in_specs=[
            pl.BlockSpec(memory_space=pltpu.SMEM),
            block(wide, half),
            block(half, wide),
            block(half, wide),
            block(half, half * half),
            pl.BlockSpec((half * wide, wide), lambda t: (0, 0)),
        ],
        out_specs=[block(half, half), block(half, half)],
        out_shape=[pair, pair],
        scratch_shapes=[
            pltpu.VMEM((half * half // 2, 2 * wide), jnp.bfloat16),
            pltpu.VMEM((2, half * half // 2, wide), jnp.float32),
            pltpu.VMEM((wide, 16 * wide), jnp.bfloat16),
            pltpu.VMEM((half, wide), jnp.float32),
        ],
        compiler_params=pltpu.CompilerParams(vmem_limit_bytes=40 * 1024 * 1024),
        name="contract",
    )(weights, turned, second, third_vecs, cubic, picker)


def look_up(table_rows, queries):
    looked_values = jnp.take(table_rows, queries.reshape(-1), axis=0)
    return looked_values.reshape(queries.shape + table_rows.shape[1:])


def exchange(value, axes):
    return lax.all_to_all(value, axes, split_axis=0, concat_axis=0, tiled=True)


def body(eigvecs, cubic, triplets, weights, deviation, source, base_rate):
    trip_count = lax.axis_size("trip")
    row_count = lax.axis_size("row")
    devices = trip_count * row_count
    everyone = ("trip", "row")
    home_rows = eigvecs.shape[0]
    branches = eigvecs.shape[1]
    trip_local = cubic.shape[0]
    columns = deviation.shape[1] // branches
    vec_size = 2 * branches * branches
    far_cap = (2 * trip_local + devices - 1) // devices
    row_cap = trip_local // 2
    row_slots = row_count * row_cap
    home_dev = triplets[:, 0] // home_rows
    row_target = home_dev % row_count
    row_place = row_target * row_cap + ranks_of(row_target)
    row_local = triplets[:, 0] - home_dev * home_rows
    row_code = pack_ints(row_place, row_local + 1, row_slots).reshape(row_count, row_cap)
    far_index = triplets[:, 1:].reshape(-1)
    far_owner = far_index // home_rows
    far_place = far_owner * far_cap + ranks_of(far_owner)
    far_queries = pack_ints(
        far_place, far_index - far_owner * home_rows, devices * far_cap
    ).reshape(devices, far_cap)
    arrived_codes = exchange(row_code, "row")
    queries_here = exchange(far_queries, everyone)
    flat_vecs = eigvecs.reshape(home_rows, vec_size)
    row_found = exchange(look_up(flat_vecs, jnp.maximum(arrived_codes - 1, 0)), "row")
    first_vecs = jnp.take(row_found.reshape(row_slots, vec_size), row_place, axis=0)
    far_table = jnp.concatenate([flat_vecs, deviation.astype(jnp.bfloat16)], 1)
    far_found = exchange(look_up(far_table, queries_here), everyone)
    far_found = jnp.take(far_found.reshape(devices * far_cap, -1), far_place, axis=0)
    far_vecs = far_found[:, :vec_size].reshape(trip_local, 2, branches, 2 * branches)
    states = far_found[:, vec_size:]
    first_pairing, second_pairing = contract_all(
        cubic,
        first_vecs.reshape(trip_local, branches, 2 * branches),
        far_vecs[:, 0],
        far_vecs[:, 1],
        weights,
    )
    pairing = jnp.concatenate([first_pairing, second_pairing], 2)
    rates = jnp.sum(pairing.astype(jnp.float32), 2)
    highest = lax.Precision.HIGHEST
    onehot = (
        lax.broadcasted_iota(jnp.int32, (home_rows, row_slots), 0)
        == arrived_codes.reshape(-1)[None, :] - 1
    ).astype(jnp.float32)
    phonon_state = deviation.reshape(home_rows, branches, columns)
    driven = source.reshape(home_rows, branches, columns)
    for update in range(ITERS):
        if update > 0:
            outgoing = phonon_state.reshape(home_rows, branches * columns).astype(jnp.bfloat16)
            states = exchange(look_up(outgoing, queries_here), everyone)
            states = jnp.take(states.reshape(devices * far_cap, -1), far_place, axis=0)
        terms = jnp.einsum(
            "tab,tbc->tac",
            pairing,
            states.reshape(trip_local, 2 * branches, columns),
            preferred_element_type=jnp.float32,
        ).reshape(trip_local, branches * columns)
        if update == 0:
            terms = jnp.concatenate([rates, terms], 1)
        packed = pack_rows(row_place, terms, row_slots)
        arrived = exchange(packed.reshape(row_count, row_cap, -1), "row")
        summed = jnp.dot(
            onehot,
            arrived.reshape(row_slots, -1),
            preferred_element_type=jnp.float32,
            precision=highest,
        )
        if update == 0:
            total_rate = base_rate + summed[:, :branches]
            summed = summed[:, branches:]
        coupled = summed.reshape(home_rows, branches, columns)
        phonon_state = (1.0 - damping) * phonon_state + damping * (
            driven + coupled
        ) / total_rate[:, :, None]
    return phonon_state.reshape(home_rows, branches * columns)


def solution(mesh):
    in_specs = (
        P(("trip", "row"), None, None),
        P(("trip", "row"), None, None),
        P(("trip", "row"), None),
        P(("trip", "row")),
        P(("trip", "row"), None),
        P(("trip", "row"), None),
        P(("trip", "row"), None),
    )
    out_specs = P(("trip", "row"), None)
    return jax.shard_map(body, mesh=mesh, in_specs=in_specs, out_specs=out_specs, check_vma=False)
```

```python
import jax
import jax.numpy as jnp
from jax import lax
from jax.experimental import pallas as pl
from jax.experimental.pallas import tpu as pltpu
from jax.sharding import PartitionSpec as P

ITERS = 2
BRANCHES = 64


damping = 0.7


def ranks_of(target):
    chain_length = target.shape[0]
    matches = target[:, None] == target[None, :]
    earlier = lax.broadcasted_iota(
        jnp.int32, (chain_length, chain_length), 1
    ) < lax.broadcasted_iota(jnp.int32, (chain_length, chain_length), 0)
    return jnp.sum((matches & earlier).astype(jnp.int32), axis=1)


def slot_onehot(places, extent):
    return lax.broadcasted_iota(jnp.int32, (extent, places.shape[0]), 0) == places[None, :]


def pack_ints(places, values, extent):
    return jnp.sum(jnp.where(slot_onehot(places, extent), values[None, :], 0), axis=1)


def pack_rows(places, values, extent):
    onehot = slot_onehot(places, extent).astype(values.dtype)
    packed = jnp.dot(
        onehot, values, preferred_element_type=jnp.float32, precision=lax.Precision.HIGHEST
    )
    return packed.astype(values.dtype)


def first_kernel(place_ref, first_ref, cubic_ref, stacked_ref):
    half = BRANCHES
    wide = 2 * BRANCHES
    turned = first_ref[0].astype(jnp.float32).T.astype(jnp.bfloat16)
    step = 1024
    for start in range(0, BRANCHES * BRANCHES, step):
        part = jnp.dot(
            turned, cubic_ref[0, :, start : start + step], preferred_element_type=jnp.float32
        ).astype(jnp.bfloat16)
        for offset in range(0, step, wide):
            row = (start + offset) // wide * half
            stacked_ref[0, row : row + half, :wide] = part[:half, offset : offset + wide]
            stacked_ref[0, row : row + half, wide:] = part[half:, offset : offset + wide]


def contract_first(cubic, row_table, row_place):
    count = cubic.shape[0]
    half = BRANCHES
    rows = half * half // 2
    return pl.pallas_call(
        first_kernel,
        grid_spec=pltpu.PrefetchScalarGridSpec(
            num_scalar_prefetch=1,
            grid=(count,),
            in_specs=[
                pl.BlockSpec((1, half, 2 * half), lambda t, place: (place[t], 0, 0)),
                pl.BlockSpec((1, half, half * half), lambda t, place: (t, 0, 0)),
            ],
            out_specs=pl.BlockSpec((1, rows, 4 * half), lambda t, place: (t, 0, 0)),
        ),
        out_shape=jax.ShapeDtypeStruct((count, rows, 4 * half), jnp.bfloat16),
        compiler_params=pltpu.CompilerParams(vmem_limit_bytes=60 * 1024 * 1024),
        cost_estimate=pl.CostEstimate(
            flops=count * 4 * half**4, bytes_accessed=count * 6 * half**3, transcendentals=0
        ),
        name="contract_first",
    )(row_place, row_table, cubic)


def rest_kernel(place_ref, weight_ref, second_ref, third_ref, stacked_ref,
                pair_one_ref, pair_two_ref, picker, middle, spread, column_sums, loose):
    half = BRANCHES
    wide = 2 * BRANCHES
    pairs = BRANCHES // 2
    lane = lax.broadcasted_iota(jnp.int32, (1, wide), 1)
    sign = jnp.where(lane < half, -1.0, 1.0)

    @pl.when(pl.program_id(0) == 0)
    def _():
        for a in range(half):
            chosen = lax.broadcasted_iota(jnp.int32, (wide, wide), 1) == a
            picker[a * wide : (a + 1) * wide, :] = jnp.where(chosen, 1.0, 0.0).astype(
                jnp.bfloat16
            )

    loose[...] = second_ref[0, :half].astype(jnp.float32)
    second = jnp.concatenate(
        [loose[pl.ds(0, pairs, stride=2), :], loose[pl.ds(1, pairs, stride=2), :]], 0
    ).T
    second = jnp.concatenate([second[:half], second[half:]], 1).astype(jnp.bfloat16)
    third = third_ref[0, :half]
    swapped = (pltpu.roll(third.astype(jnp.float32), half, 1) * sign).astype(jnp.bfloat16)
    zero = jnp.zeros_like(third)
    mixer = jnp.concatenate(
        [
            jnp.concatenate([third, zero, swapped, zero], 0),
            jnp.concatenate([zero, third, zero, swapped], 0),
        ],
        1,
    )
    for start in range(0, pairs * half, 256):
        part = jnp.dot(
            stacked_ref[0, start : start + 256, :], mixer, preferred_element_type=jnp.float32
        )
        middle[0, start : start + 256, :] = part[:, :wide]
        middle[1, start : start + 256, :] = part[:, wide:]
    group = 8
    total = jnp.zeros((half, wide), jnp.float32)
    for first in range(0, half, group):
        for a in range(first, first + group):
            place = (a % (2 * group)) * wide
            for side in range(2):
                value = middle[side, pl.ds(a, pairs, stride=half), :]
                turned = pltpu.roll(value, half, 1) * sign
                low = side * pairs
                spread[low : low + pairs, place : place + wide] = value.astype(jnp.bfloat16)
                spread[half + low : half + low + pairs, place : place + wide] = turned.astype(
                    jnp.bfloat16
                )
        begin = (first % (2 * group)) * wide
        found = jnp.dot(
            second, spread[:, begin : begin + group * wide], preferred_element_type=jnp.float32
        )
        square = found * found
        total = total + jnp.dot(
            square.astype(jnp.bfloat16),
            picker[first * wide : (first + group) * wide, :],
            preferred_element_type=jnp.float32,
        )
        sums = jnp.sum(square, 0, keepdims=True)
        column_sums[first : first + group, :] = jnp.concatenate(
            [sums[:, q * wide : (q + 1) * wide] for q in range(group)], 0
        )
    weight = weight_ref[pl.program_id(0)].astype(jnp.float32)
    full = column_sums[...]
    full = (full + pltpu.roll(full, half, 1)) * weight
    pair_one_ref[0] = (total * weight).T[:half].astype(jnp.bfloat16)
    pair_two_ref[0] = full[:, :half].astype(jnp.bfloat16)


def contract_rest(stacked, far_table, far_place, weights):
    count = stacked.shape[0]
    half = BRANCHES
    wide = 2 * half
    rows = half * half // 2
    slab = far_table.shape[1]

    def block(*shape):
        return pl.BlockSpec((1,) + shape, lambda t, place, weight: (t, 0, 0))

    pair = jax.ShapeDtypeStruct((count, half, half), jnp.bfloat16)
    return pl.pallas_call(
        rest_kernel,
        grid_spec=pltpu.PrefetchScalarGridSpec(
            num_scalar_prefetch=2,
            grid=(count,),
            in_specs=[
                pl.BlockSpec((1, slab, wide), lambda t, place, weight: (place[2 * t], 0, 0)),
                pl.BlockSpec((1, slab, wide), lambda t, place, weight: (place[2 * t + 1], 0, 0)),
                block(rows, 2 * wide),
            ],
            out_specs=[block(half, half), block(half, half)],
            scratch_shapes=[
                pltpu.VMEM((half * wide, wide), jnp.bfloat16),
                pltpu.VMEM((2, rows, wide), jnp.float32),
                pltpu.VMEM((wide, 16 * wide), jnp.bfloat16),
                pltpu.VMEM((half, wide), jnp.float32),
                pltpu.VMEM((half, wide), jnp.float32),
            ],
        ),
        out_shape=[pair, pair],
        compiler_params=pltpu.CompilerParams(vmem_limit_bytes=40 * 1024 * 1024),
        name="contract_rest",
    )(far_place, weights, far_table, far_table, stacked)


def swap_kernel(in_ref, out_ref, send_sem, recv_sem, local_sem):
    count = in_ref.shape[0]
    trip = lax.axis_index("trip")
    me = lax.axis_index("row")
    barrier = pltpu.get_barrier_semaphore()
    for away in range(1, count):
        peer = lax.rem(me + away, count)
        pl.semaphore_signal(
            barrier, inc=1, device_id=(trip, peer), device_id_type=pl.DeviceIdType.MESH
        )
    pl.semaphore_wait(barrier, count - 1)
    copies = []
    for away in range(1, count):
        peer = lax.rem(me + away, count)
        copy = pltpu.make_async_remote_copy(
            src_ref=in_ref.at[peer],
            dst_ref=out_ref.at[me],
            send_sem=send_sem.at[away - 1],
            recv_sem=recv_sem.at[away - 1],
            device_id=(trip, peer),
            device_id_type=pl.DeviceIdType.MESH,
        )
        copy.start()
        copies.append(copy)
    own = pltpu.make_async_copy(in_ref.at[me], out_ref.at[me], local_sem)
    own.start()
    own.wait()
    for copy in copies:
        copy.wait()


def row_swap(value, number):
    return pl.pallas_call(
        swap_kernel,
        in_specs=[pl.BlockSpec(memory_space=pltpu.VMEM)],
        out_specs=pl.BlockSpec(memory_space=pltpu.VMEM),
        out_shape=jax.ShapeDtypeStruct(value.shape, value.dtype),
        scratch_shapes=[
            pltpu.SemaphoreType.DMA((value.shape[0] - 1,)),
            pltpu.SemaphoreType.DMA((value.shape[0] - 1,)),
            pltpu.SemaphoreType.DMA,
        ],
        compiler_params=pltpu.CompilerParams(collective_id=number, has_side_effects=True),
        cost_estimate=pl.CostEstimate(flops=0, bytes_accessed=8 * value.size, transcendentals=0),
        name="row_swap",
    )(value)


def look_up(table_rows, queries):
    looked_values = jnp.take(table_rows, queries.reshape(-1), axis=0)
    return looked_values.reshape(queries.shape + table_rows.shape[1:])


def exchange(value, axes):
    return lax.all_to_all(value, axes, split_axis=0, concat_axis=0, tiled=True)


def body(eigvecs, cubic, triplets, weights, deviation, source, base_rate):
    trip_count = lax.axis_size("trip")
    row_count = lax.axis_size("row")
    devices = trip_count * row_count
    everyone = ("trip", "row")
    home_rows = eigvecs.shape[0]
    branches = eigvecs.shape[1]
    trip_local = cubic.shape[0]
    columns = deviation.shape[1] // branches
    far_size = branches * columns
    slab_rows = far_size // (2 * branches)
    row_cap = trip_local // 2
    row_slots = row_count * row_cap
    home_dev = triplets[:, 0] // home_rows
    row_target = home_dev % row_count
    row_place = row_target * row_cap + ranks_of(row_target)
    row_local = triplets[:, 0] - home_dev * home_rows
    row_code = pack_ints(row_place, row_local + 1, row_slots).reshape(row_count, 1, row_cap)
    far_index = triplets[:, 1:].reshape(-1)
    far_place = far_index // home_rows
    far_queries = jnp.max(
        jnp.where(
            slot_onehot(far_place, devices), (far_index - far_place * home_rows)[None, :], 0
        ),
        axis=1,
    )
    arrived_codes = row_swap(row_code, 2).reshape(row_count, row_cap)
    queries_here = exchange(far_queries, everyone)
    row_table = row_swap(look_up(eigvecs, jnp.maximum(arrived_codes - 1, 0)), 3)
    row_table = row_table.reshape((row_slots,) + eigvecs.shape[1:])
    sent = deviation.astype(jnp.bfloat16).reshape(home_rows, slab_rows, 2 * branches)
    slab = jnp.concatenate(
        [eigvecs, sent, jnp.zeros((home_rows, -slab_rows % 8, 2 * branches), jnp.bfloat16)], 1
    )
    far_table = exchange(look_up(slab, queries_here), everyone)
    stacked = contract_first(cubic, row_table, row_place)
    states = far_table[:, branches : branches + slab_rows].reshape(devices, far_size)
    states = jnp.take(states, far_place, axis=0)
    first_pairing, second_pairing = contract_rest(stacked, far_table, far_place, weights)
    pairing = jnp.concatenate([first_pairing, second_pairing], 2)
    rates = jnp.sum(pairing.astype(jnp.float32), 2)
    highest = lax.Precision.HIGHEST
    onehot = (
        lax.broadcasted_iota(jnp.int32, (home_rows, row_slots), 0)
        == arrived_codes.reshape(-1)[None, :] - 1
    ).astype(jnp.float32)
    phonon_state = deviation.reshape(home_rows, branches, columns)
    driven = source.reshape(home_rows, branches, columns)
    for update in range(ITERS):
        if update > 0:
            outgoing = phonon_state.reshape(home_rows, branches * columns).astype(jnp.bfloat16)
            states = exchange(look_up(outgoing, queries_here), everyone)
            states = jnp.take(states, far_place, axis=0)
        terms = jnp.einsum(
            "tab,tbc->tac",
            pairing,
            states.reshape(trip_local, 2 * branches, columns),
            preferred_element_type=jnp.float32,
        ).reshape(trip_local, branches * columns)
        if update == 0:
            terms = jnp.concatenate([rates, terms], 1)
        packed = pack_rows(row_place, terms, row_slots)
        arrived = row_swap(packed.reshape(row_count, row_cap, -1), update)
        summed = jnp.dot(
            onehot,
            arrived.reshape(row_slots, -1),
            preferred_element_type=jnp.float32,
            precision=highest,
        )
        if update == 0:
            total_rate = base_rate + summed[:, :branches]
            summed = summed[:, branches:]
        coupled = summed.reshape(home_rows, branches, columns)
        phonon_state = (1.0 - damping) * phonon_state + damping * (
            driven + coupled
        ) / total_rate[:, :, None]
    return phonon_state.reshape(home_rows, branches * columns)


def solution(mesh):
    in_specs = (
        P(("trip", "row"), None, None),
        P(("trip", "row"), None, None),
        P(("trip", "row"), None),
        P(("trip", "row")),
        P(("trip", "row"), None),
        P(("trip", "row"), None),
        P(("trip", "row"), None),
    )
    out_specs = P(("trip", "row"), None)
    return jax.shard_map(body, mesh=mesh, in_specs=in_specs, out_specs=out_specs, check_vma=False)
```

```python
import jax
import jax.numpy as jnp
from jax import lax
from jax.experimental import pallas as pl
from jax.experimental.pallas import tpu as pltpu
from jax.sharding import PartitionSpec as P

ITERS = 2
BRANCHES = 64


damping = 0.7


def ranks_of(target):
    chain_length = target.shape[0]
    matches = target[:, None] == target[None, :]
    earlier = lax.broadcasted_iota(
        jnp.int32, (chain_length, chain_length), 1
    ) < lax.broadcasted_iota(jnp.int32, (chain_length, chain_length), 0)
    return jnp.sum((matches & earlier).astype(jnp.int32), axis=1)


def slot_onehot(places, extent):
    return lax.broadcasted_iota(jnp.int32, (extent, places.shape[0]), 0) == places[None, :]


def pack_ints(places, values, extent):
    return jnp.sum(jnp.where(slot_onehot(places, extent), values[None, :], 0), axis=1)


def pack_rows(places, values, extent):
    onehot = slot_onehot(places, extent).astype(values.dtype)
    packed = jnp.dot(
        onehot, values, preferred_element_type=jnp.float32, precision=lax.Precision.HIGHEST
    )
    return packed.astype(values.dtype)


def first_kernel(place_ref, first_ref, cubic_ref, stacked_ref):
    half = BRANCHES
    wide = 2 * BRANCHES
    turned = first_ref[0].astype(jnp.float32).T.astype(jnp.bfloat16)
    step = 1024
    for start in range(0, BRANCHES * BRANCHES, step):
        part = jnp.dot(
            turned, cubic_ref[0, :, start : start + step], preferred_element_type=jnp.float32
        ).astype(jnp.bfloat16)
        for offset in range(0, step, wide):
            row = (start + offset) // wide * half
            stacked_ref[0, row : row + half, :wide] = part[:half, offset : offset + wide]
            stacked_ref[0, row : row + half, wide:] = part[half:, offset : offset + wide]


def contract_first(cubic, row_table, row_place):
    count = cubic.shape[0]
    half = BRANCHES
    rows = half * half // 2
    return pl.pallas_call(
        first_kernel,
        grid_spec=pltpu.PrefetchScalarGridSpec(
            num_scalar_prefetch=1,
            grid=(count,),
            in_specs=[
                pl.BlockSpec((1, half, 2 * half), lambda t, place: (place[t], 0, 0)),
                pl.BlockSpec((1, half, half * half), lambda t, place: (t, 0, 0)),
            ],
            out_specs=pl.BlockSpec((1, rows, 4 * half), lambda t, place: (t, 0, 0)),
        ),
        out_shape=jax.ShapeDtypeStruct((count, rows, 4 * half), jnp.bfloat16),
        compiler_params=pltpu.CompilerParams(vmem_limit_bytes=60 * 1024 * 1024),
        cost_estimate=pl.CostEstimate(
            flops=count * 4 * half**4, bytes_accessed=count * 6 * half**3, transcendentals=0
        ),
        name="contract_first",
    )(row_place, row_table, cubic)


def rest_kernel(place_ref, weight_ref, second_ref, third_ref, stacked_ref,
                pair_one_ref, pair_two_ref, turner, spread, column_sums, loose):
    half = BRANCHES
    wide = 2 * BRANCHES
    pairs = BRANCHES // 2
    lane = lax.broadcasted_iota(jnp.int32, (1, wide), 1)
    sign = jnp.where(lane < half, -1.0, 1.0)

    @pl.when(pl.program_id(0) == 0)
    def _():
        across = lax.broadcasted_iota(jnp.int32, (4 * half, 4 * half), 0)
        along = lax.broadcasted_iota(jnp.int32, (4 * half, 4 * half), 1)
        chosen = along == (across % 16) * 16 + across // 16
        turner[...] = jnp.where(chosen, 1.0, 0.0).astype(jnp.bfloat16)

    loose[...] = second_ref[0, :half].astype(jnp.float32)
    second = jnp.concatenate(
        [loose[pl.ds(0, pairs, stride=2), :], loose[pl.ds(1, pairs, stride=2), :]], 0
    ).T
    second = jnp.concatenate([second[:half], second[half:]], 1).astype(jnp.bfloat16)
    third = third_ref[0, :half]
    swapped = (pltpu.roll(third.astype(jnp.float32), half, 1) * sign).astype(jnp.bfloat16)
    zero = jnp.zeros_like(third)

    def paired(real_rows, imag_rows):
        return jnp.concatenate(
            [
                jnp.concatenate([real_rows, zero, imag_rows, zero], 0),
                jnp.concatenate([zero, real_rows, zero, imag_rows], 0),
            ],
            1,
        )

    mixer = paired(third, swapped)
    mixer_swapped = paired(swapped, -third)
    tile = 16
    group = 8
    total = jnp.zeros((half, wide), jnp.float32)
    for first in range(0, half, tile):
        slot = first // tile % 2
        for low in range(0, pairs, tile):
            block = jnp.concatenate(
                [
                    stacked_ref[0, p * half + first : p * half + first + tile, :]
                    for p in range(low, low + tile)
                ],
                0,
            )
            block = jnp.dot(turner[...], block, preferred_element_type=jnp.float32)
            block = block.astype(jnp.bfloat16)
            plain = jnp.dot(block, mixer, preferred_element_type=jnp.float32).astype(jnp.bfloat16)
            other = jnp.dot(block, mixer_swapped, preferred_element_type=jnp.float32).astype(
                jnp.bfloat16
            )
            for side in range(2):
                value = plain[:, side * wide : (side + 1) * wide]
                turned = other[:, side * wide : (side + 1) * wide]
                row = side * pairs + low
                for a in range(tile):
                    place = slice(a * wide, (a + 1) * wide)
                    chosen = slice(a * tile, (a + 1) * tile)
                    spread[slot, row : row + tile, place] = value[chosen]
                    spread[slot, half + row : half + row + tile, place] = turned[chosen]
        for part in range(0, tile, group):
            found = jnp.dot(
                second, spread[slot, :, part * wide : (part + group) * wide],
                preferred_element_type=jnp.float32,
            )
            square = found * found
            begin = first + part
            for q in range(group):
                over = jnp.sum(square[:, q * wide : (q + 1) * wide], 1, keepdims=True)
                total = jnp.where(lane == begin + q, over, total)
            sums = jnp.sum(square, 0, keepdims=True)
            column_sums[begin : begin + group, :] = jnp.concatenate(
                [sums[:, q * wide : (q + 1) * wide] for q in range(group)], 0
            )
    weight = weight_ref[pl.program_id(0)].astype(jnp.float32)
    full = column_sums[...]
    full = (full + pltpu.roll(full, half, 1)) * weight
    pair_one_ref[0] = (total * weight).T[:half].astype(jnp.bfloat16)
    pair_two_ref[0] = full[:, :half].astype(jnp.bfloat16)


def contract_rest(stacked, far_table, far_place, weights):
    count = stacked.shape[0]
    half = BRANCHES
    wide = 2 * half
    rows = half * half // 2
    slab = far_table.shape[1]

    def block(*shape):
        return pl.BlockSpec((1,) + shape, lambda t, place, weight: (t, 0, 0))

    pair = jax.ShapeDtypeStruct((count, half, half), jnp.bfloat16)
    return pl.pallas_call(
        rest_kernel,
        grid_spec=pltpu.PrefetchScalarGridSpec(
            num_scalar_prefetch=2,
            grid=(count,),
            in_specs=[
                pl.BlockSpec((1, slab, wide), lambda t, place, weight: (place[2 * t], 0, 0)),
                pl.BlockSpec((1, slab, wide), lambda t, place, weight: (place[2 * t + 1], 0, 0)),
                block(rows, 2 * wide),
            ],
            out_specs=[block(half, half), block(half, half)],
            scratch_shapes=[
                pltpu.VMEM((2 * wide, 2 * wide), jnp.bfloat16),
                pltpu.VMEM((2, wide, 16 * wide), jnp.bfloat16),
                pltpu.VMEM((half, wide), jnp.float32),
                pltpu.VMEM((half, wide), jnp.float32),
            ],
        ),
        out_shape=[pair, pair],
        compiler_params=pltpu.CompilerParams(vmem_limit_bytes=40 * 1024 * 1024),
        name="contract_rest",
    )(far_place, weights, far_table, far_table, stacked)


def swap_kernel(in_ref, out_ref, send_sem, recv_sem, local_sem):
    count = in_ref.shape[0]
    trip = lax.axis_index("trip")
    me = lax.axis_index("row")
    barrier = pltpu.get_barrier_semaphore()
    for away in range(1, count):
        peer = lax.rem(me + away, count)
        pl.semaphore_signal(
            barrier, inc=1, device_id=(trip, peer), device_id_type=pl.DeviceIdType.MESH
        )
    pl.semaphore_wait(barrier, count - 1)
    copies = []
    for away in range(1, count):
        peer = lax.rem(me + away, count)
        copy = pltpu.make_async_remote_copy(
            src_ref=in_ref.at[peer],
            dst_ref=out_ref.at[me],
            send_sem=send_sem.at[away - 1],
            recv_sem=recv_sem.at[away - 1],
            device_id=(trip, peer),
            device_id_type=pl.DeviceIdType.MESH,
        )
        copy.start()
        copies.append(copy)
    own = pltpu.make_async_copy(in_ref.at[me], out_ref.at[me], local_sem)
    own.start()
    own.wait()
    for copy in copies:
        copy.wait()


def row_swap(value, number):
    return pl.pallas_call(
        swap_kernel,
        in_specs=[pl.BlockSpec(memory_space=pltpu.VMEM)],
        out_specs=pl.BlockSpec(memory_space=pltpu.VMEM),
        out_shape=jax.ShapeDtypeStruct(value.shape, value.dtype),
        scratch_shapes=[
            pltpu.SemaphoreType.DMA((value.shape[0] - 1,)),
            pltpu.SemaphoreType.DMA((value.shape[0] - 1,)),
            pltpu.SemaphoreType.DMA,
        ],
        compiler_params=pltpu.CompilerParams(collective_id=number, has_side_effects=True),
        cost_estimate=pl.CostEstimate(flops=0, bytes_accessed=8 * value.size, transcendentals=0),
        name="row_swap",
    )(value)


def look_up(table_rows, queries):
    looked_values = jnp.take(table_rows, queries.reshape(-1), axis=0)
    return looked_values.reshape(queries.shape + table_rows.shape[1:])


def exchange(value, axes):
    return lax.all_to_all(value, axes, split_axis=0, concat_axis=0, tiled=True)


def body(eigvecs, cubic, triplets, weights, deviation, source, base_rate):
    trip_count = lax.axis_size("trip")
    row_count = lax.axis_size("row")
    devices = trip_count * row_count
    everyone = ("trip", "row")
    home_rows = eigvecs.shape[0]
    branches = eigvecs.shape[1]
    trip_local = cubic.shape[0]
    columns = deviation.shape[1] // branches
    far_size = branches * columns
    slab_rows = far_size // (2 * branches)
    row_cap = trip_local // 2
    row_slots = row_count * row_cap
    home_dev = triplets[:, 0] // home_rows
    row_target = home_dev % row_count
    row_place = row_target * row_cap + ranks_of(row_target)
    row_local = triplets[:, 0] - home_dev * home_rows
    row_code = pack_ints(row_place, row_local + 1, row_slots).reshape(row_count, 1, row_cap)
    far_index = triplets[:, 1:].reshape(-1)
    far_place = far_index // home_rows
    far_queries = jnp.max(
        jnp.where(
            slot_onehot(far_place, devices), (far_index - far_place * home_rows)[None, :], 0
        ),
        axis=1,
    )
    arrived_codes = row_swap(row_code, 2).reshape(row_count, row_cap)
    queries_here = exchange(far_queries, everyone)
    row_table = row_swap(look_up(eigvecs, jnp.maximum(arrived_codes - 1, 0)), 3)
    row_table = row_table.reshape((row_slots,) + eigvecs.shape[1:])
    sent = deviation.astype(jnp.bfloat16).reshape(home_rows, slab_rows, 2 * branches)
    slab = jnp.concatenate(
        [eigvecs, sent, jnp.zeros((home_rows, -slab_rows % 8, 2 * branches), jnp.bfloat16)], 1
    )
    row_table, outgoing = lax.optimization_barrier((row_table, look_up(slab, queries_here)))
    far_table = exchange(outgoing, everyone)
    stacked = contract_first(cubic, row_table, row_place)
    states = far_table[:, branches : branches + slab_rows].reshape(devices, far_size)
    states = jnp.take(states, far_place, axis=0)
    first_pairing, second_pairing = contract_rest(stacked, far_table, far_place, weights)
    pairing = jnp.concatenate([first_pairing, second_pairing], 2)
    rates = jnp.sum(pairing.astype(jnp.float32), 2)
    highest = lax.Precision.HIGHEST
    onehot = (
        lax.broadcasted_iota(jnp.int32, (home_rows, row_slots), 0)
        == arrived_codes.reshape(-1)[None, :] - 1
    ).astype(jnp.float32)
    phonon_state = deviation.reshape(home_rows, branches, columns)
    driven = source.reshape(home_rows, branches, columns)
    for update in range(ITERS):
        if update > 0:
            outgoing = phonon_state.astype(jnp.bfloat16).reshape(sent.shape)
            states = exchange(look_up(outgoing, queries_here), everyone)
            states = states.reshape(devices, far_size)
            states = jnp.take(states, far_place, axis=0)
        terms = jnp.einsum(
            "tab,tbc->tac",
            pairing,
            states.reshape(trip_local, 2 * branches, columns),
            preferred_element_type=jnp.float32,
        ).reshape(trip_local, branches * columns)
        if update == 0:
            terms = jnp.concatenate([rates, terms], 1)
        packed = pack_rows(row_place, terms, row_slots)
        arrived = row_swap(packed.reshape(row_count, row_cap, -1), update)
        summed = jnp.dot(
            onehot,
            arrived.reshape(row_slots, -1),
            preferred_element_type=jnp.float32,
            precision=highest,
        )
        if update == 0:
            total_rate = base_rate + summed[:, :branches]
            summed = summed[:, branches:]
        coupled = summed.reshape(home_rows, branches, columns)
        phonon_state = (1.0 - damping) * phonon_state + damping * (
            driven + coupled
        ) / total_rate[:, :, None]
    return phonon_state.reshape(home_rows, branches * columns)


def solution(mesh):
    in_specs = (
        P(("trip", "row"), None, None),
        P(("trip", "row"), None, None),
        P(("trip", "row"), None),
        P(("trip", "row")),
        P(("trip", "row"), None),
        P(("trip", "row"), None),
        P(("trip", "row"), None),
    )
    out_specs = P(("trip", "row"), None)
    return jax.shard_map(body, mesh=mesh, in_specs=in_specs, out_specs=out_specs, check_vma=False)
```

```python
import jax
import jax.numpy as jnp
from jax import lax
from jax.experimental import pallas as pl
from jax.experimental.pallas import tpu as pltpu
from jax.sharding import PartitionSpec as P

ITERS = 2
BRANCHES = 64


damping = 0.7


def ranks_of(target):
    chain_length = target.shape[0]
    matches = target[:, None] == target[None, :]
    earlier = lax.broadcasted_iota(
        jnp.int32, (chain_length, chain_length), 1
    ) < lax.broadcasted_iota(jnp.int32, (chain_length, chain_length), 0)
    return jnp.sum((matches & earlier).astype(jnp.int32), axis=1)


def slot_onehot(places, extent):
    return lax.broadcasted_iota(jnp.int32, (extent, places.shape[0]), 0) == places[None, :]


def pack_ints(places, values, extent):
    return jnp.sum(jnp.where(slot_onehot(places, extent), values[None, :], 0), axis=1)


def pack_rows(places, values, extent):
    onehot = slot_onehot(places, extent).astype(values.dtype)
    packed = jnp.dot(
        onehot, values, preferred_element_type=jnp.float32, precision=lax.Precision.HIGHEST
    )
    return packed.astype(values.dtype)


def first_kernel(place_ref, first_ref, cubic_ref, stacked_ref):
    half = BRANCHES
    wide = 2 * BRANCHES
    turned = first_ref[0].astype(jnp.float32).T.astype(jnp.bfloat16)
    step = 1024
    for start in range(0, BRANCHES * BRANCHES, step):
        part = jnp.dot(
            turned, cubic_ref[0, :, start : start + step], preferred_element_type=jnp.float32
        ).astype(jnp.bfloat16)
        for offset in range(0, step, wide):
            row = (start + offset) // wide * half
            stacked_ref[0, row : row + half, :wide] = part[:half, offset : offset + wide]
            stacked_ref[0, row : row + half, wide:] = part[half:, offset : offset + wide]


def contract_first(cubic, row_table, row_place):
    count = cubic.shape[0]
    half = BRANCHES
    rows = half * half // 2
    return pl.pallas_call(
        first_kernel,
        grid_spec=pltpu.PrefetchScalarGridSpec(
            num_scalar_prefetch=1,
            grid=(count,),
            in_specs=[
                pl.BlockSpec((1, half, 2 * half), lambda t, place: (place[t], 0, 0)),
                pl.BlockSpec((1, half, half * half), lambda t, place: (t, 0, 0)),
            ],
            out_specs=pl.BlockSpec((1, rows, 4 * half), lambda t, place: (t, 0, 0)),
        ),
        out_shape=jax.ShapeDtypeStruct((count, rows, 4 * half), jnp.bfloat16),
        compiler_params=pltpu.CompilerParams(vmem_limit_bytes=60 * 1024 * 1024),
        cost_estimate=pl.CostEstimate(
            flops=count * 4 * half**4, bytes_accessed=count * 6 * half**3, transcendentals=0
        ),
        name="contract_first",
    )(row_place, row_table, cubic)


def rest_kernel(place_ref, weight_ref, second_ref, third_ref, stacked_ref,
                pair_one_ref, pair_two_ref, turner, spread, column_sums, loose):
    half = BRANCHES
    wide = 2 * BRANCHES
    pairs = BRANCHES // 2
    lane = lax.broadcasted_iota(jnp.int32, (1, wide), 1)
    sign = jnp.where(lane < half, -1.0, 1.0)

    @pl.when(pl.program_id(0) == 0)
    def _():
        across = lax.broadcasted_iota(jnp.int32, (4 * half, 4 * half), 0)
        along = lax.broadcasted_iota(jnp.int32, (4 * half, 4 * half), 1)
        chosen = along == (across % 16) * 16 + across // 16
        turner[...] = jnp.where(chosen, 1.0, 0.0).astype(jnp.bfloat16)

    loose[...] = second_ref[0, :half].astype(jnp.float32)
    second = jnp.concatenate(
        [loose[pl.ds(0, pairs, stride=2), :], loose[pl.ds(1, pairs, stride=2), :]], 0
    ).T
    second = jnp.concatenate([second[:half], second[half:]], 1).astype(jnp.bfloat16)
    third = third_ref[0, :half]
    swapped = (pltpu.roll(third.astype(jnp.float32), half, 1) * sign).astype(jnp.bfloat16)
    zero = jnp.zeros_like(third)

    def paired(real_rows, imag_rows):
        return jnp.concatenate(
            [
                jnp.concatenate([real_rows, zero, imag_rows, zero], 0),
                jnp.concatenate([zero, real_rows, zero, imag_rows], 0),
            ],
            1,
        )

    mixer = paired(third, swapped)
    mixer_swapped = paired(swapped, -third)
    tile = 16
    group = 8
    total = jnp.zeros((half, wide), jnp.float32)
    for first in range(0, half, tile):
        slot = first // tile % 2
        for low in range(0, pairs, tile):
            block = jnp.concatenate(
                [
                    stacked_ref[0, p * half + first : p * half + first + tile, :]
                    for p in range(low, low + tile)
                ],
                0,
            )
            block = jnp.dot(turner[...], block, preferred_element_type=jnp.float32)
            block = block.astype(jnp.bfloat16)
            plain = jnp.dot(block, mixer, preferred_element_type=jnp.float32).astype(jnp.bfloat16)
            other = jnp.dot(block, mixer_swapped, preferred_element_type=jnp.float32).astype(
                jnp.bfloat16
            )
            for side in range(2):
                value = plain[:, side * wide : (side + 1) * wide]
                turned = other[:, side * wide : (side + 1) * wide]
                row = side * pairs + low
                for a in range(tile):
                    place = slice(a * wide, (a + 1) * wide)
                    chosen = slice(a * tile, (a + 1) * tile)
                    spread[slot, row : row + tile, place] = value[chosen]
                    spread[slot, half + row : half + row + tile, place] = turned[chosen]
        for part in range(0, tile, group):
            found = jnp.dot(
                second, spread[slot, :, part * wide : (part + group) * wide],
                preferred_element_type=jnp.float32,
            )
            square = found * found
            begin = first + part
            for q in range(group):
                over = jnp.sum(square[:, q * wide : (q + 1) * wide], 1, keepdims=True)
                total = jnp.where(lane == begin + q, over, total)
            sums = jnp.sum(square, 0, keepdims=True)
            column_sums[begin : begin + group, :] = jnp.concatenate(
                [sums[:, q * wide : (q + 1) * wide] for q in range(group)], 0
            )
    weight = weight_ref[pl.program_id(0)].astype(jnp.float32)
    full = column_sums[...]
    full = (full + pltpu.roll(full, half, 1)) * weight
    pair_one_ref[0] = (total * weight).T[:half].astype(jnp.bfloat16)
    pair_two_ref[0] = full[:, :half].astype(jnp.bfloat16)


def contract_rest(stacked, far_table, far_place, weights):
    count = stacked.shape[0]
    half = BRANCHES
    wide = 2 * half
    rows = half * half // 2
    slab = far_table.shape[1]

    def block(*shape):
        return pl.BlockSpec((1,) + shape, lambda t, place, weight: (t, 0, 0))

    pair = jax.ShapeDtypeStruct((count, half, half), jnp.bfloat16)
    return pl.pallas_call(
        rest_kernel,
        grid_spec=pltpu.PrefetchScalarGridSpec(
            num_scalar_prefetch=2,
            grid=(count,),
            in_specs=[
                pl.BlockSpec((1, slab, wide), lambda t, place, weight: (place[2 * t], 0, 0)),
                pl.BlockSpec((1, slab, wide), lambda t, place, weight: (place[2 * t + 1], 0, 0)),
                block(rows, 2 * wide),
            ],
            out_specs=[block(half, half), block(half, half)],
            scratch_shapes=[
                pltpu.VMEM((2 * wide, 2 * wide), jnp.bfloat16),
                pltpu.VMEM((2, wide, 16 * wide), jnp.bfloat16),
                pltpu.VMEM((half, wide), jnp.float32),
                pltpu.VMEM((half, wide), jnp.float32),
            ],
        ),
        out_shape=[pair, pair],
        compiler_params=pltpu.CompilerParams(vmem_limit_bytes=40 * 1024 * 1024),
        name="contract_rest",
    )(far_place, weights, far_table, far_table, stacked)


def swap_kernel(in_ref, out_ref, send_sem, recv_sem, local_sem):
    count = in_ref.shape[0]
    trip = lax.axis_index("trip")
    me = lax.axis_index("row")
    barrier = pltpu.get_barrier_semaphore()
    for away in range(1, count):
        peer = lax.rem(me + away, count)
        pl.semaphore_signal(
            barrier, inc=1, device_id=(trip, peer), device_id_type=pl.DeviceIdType.MESH
        )
    pl.semaphore_wait(barrier, count - 1)
    copies = []
    for away in range(1, count):
        peer = lax.rem(me + away, count)
        copy = pltpu.make_async_remote_copy(
            src_ref=in_ref.at[peer],
            dst_ref=out_ref.at[me],
            send_sem=send_sem.at[away - 1],
            recv_sem=recv_sem.at[away - 1],
            device_id=(trip, peer),
            device_id_type=pl.DeviceIdType.MESH,
        )
        copy.start()
        copies.append(copy)
    own = pltpu.make_async_copy(in_ref.at[me], out_ref.at[me], local_sem)
    own.start()
    own.wait()
    for copy in copies:
        copy.wait()


def row_swap(value, number):
    return pl.pallas_call(
        swap_kernel,
        in_specs=[pl.BlockSpec(memory_space=pltpu.VMEM)],
        out_specs=pl.BlockSpec(memory_space=pltpu.VMEM),
        out_shape=jax.ShapeDtypeStruct(value.shape, value.dtype),
        scratch_shapes=[
            pltpu.SemaphoreType.DMA((value.shape[0] - 1,)),
            pltpu.SemaphoreType.DMA((value.shape[0] - 1,)),
            pltpu.SemaphoreType.DMA,
        ],
        compiler_params=pltpu.CompilerParams(collective_id=number, has_side_effects=True),
        cost_estimate=pl.CostEstimate(flops=0, bytes_accessed=8 * value.size, transcendentals=0),
        name="row_swap",
    )(value)


def look_up(table_rows, queries):
    looked_values = table_rows.at[queries.reshape(-1)].get(mode="promise_in_bounds")
    return looked_values.reshape(queries.shape + table_rows.shape[1:])


def exchange(value, axes):
    return lax.all_to_all(value, axes, split_axis=0, concat_axis=0, tiled=True)


def body(eigvecs, cubic, triplets, weights, deviation, source, base_rate):
    trip_count = lax.axis_size("trip")
    row_count = lax.axis_size("row")
    devices = trip_count * row_count
    everyone = ("trip", "row")
    home_rows = eigvecs.shape[0]
    branches = eigvecs.shape[1]
    trip_local = cubic.shape[0]
    columns = deviation.shape[1] // branches
    far_size = branches * columns
    slab_rows = far_size // (2 * branches)
    row_cap = trip_local // 2
    row_slots = row_count * row_cap
    home_dev = triplets[:, 0] // home_rows
    row_target = home_dev % row_count
    row_place = row_target * row_cap + ranks_of(row_target)
    row_local = triplets[:, 0] - home_dev * home_rows
    row_code = pack_ints(row_place, row_local + 1, row_slots).reshape(row_count, 1, row_cap)
    far_index = triplets[:, 1:].reshape(-1)
    far_place = far_index // home_rows
    far_queries = jnp.max(
        jnp.where(
            slot_onehot(far_place, devices), (far_index - far_place * home_rows)[None, :], 0
        ),
        axis=1,
    )
    arrived_codes = row_swap(row_code, 2).reshape(row_count, row_cap)
    queries_here = exchange(far_queries, everyone)
    row_table = row_swap(look_up(eigvecs, jnp.maximum(arrived_codes - 1, 0)), 3)
    row_table = row_table.reshape((row_slots,) + eigvecs.shape[1:])
    sent = deviation.astype(jnp.bfloat16).reshape(home_rows, slab_rows, 2 * branches)
    slab = jnp.concatenate(
        [eigvecs, sent, jnp.zeros((home_rows, -slab_rows % 8, 2 * branches), jnp.bfloat16)], 1
    )
    row_table, outgoing = lax.optimization_barrier((row_table, look_up(slab, queries_here)))
    far_table = exchange(outgoing, everyone)
    stacked = contract_first(cubic, row_table, row_place)
    states = far_table[:, branches : branches + slab_rows].reshape(devices, far_size)
    states = states.at[far_place].get(mode="promise_in_bounds")
    first_pairing, second_pairing = contract_rest(stacked, far_table, far_place, weights)
    pairing = jnp.concatenate([first_pairing, second_pairing], 2)
    rates = jnp.sum(pairing.astype(jnp.float32), 2)
    highest = lax.Precision.HIGHEST
    onehot = (
        lax.broadcasted_iota(jnp.int32, (home_rows, row_slots), 0)
        == arrived_codes.reshape(-1)[None, :] - 1
    ).astype(jnp.float32)
    phonon_state = deviation.reshape(home_rows, branches, columns)
    driven = source.reshape(home_rows, branches, columns)
    for update in range(ITERS):
        if update > 0:
            outgoing = phonon_state.astype(jnp.bfloat16).reshape(sent.shape)
            states = exchange(look_up(outgoing, queries_here), everyone)
            states = states.reshape(devices, far_size)
            states = states.at[far_place].get(mode="promise_in_bounds")
        terms = jnp.einsum(
            "tab,tbc->tac",
            pairing,
            states.reshape(trip_local, 2 * branches, columns),
            preferred_element_type=jnp.float32,
        ).reshape(trip_local, branches * columns)
        if update == 0:
            terms = jnp.concatenate([rates, terms], 1)
        packed = pack_rows(row_place, terms, row_slots)
        arrived = row_swap(packed.reshape(row_count, row_cap, -1), update)
        summed = jnp.dot(
            onehot,
            arrived.reshape(row_slots, -1),
            preferred_element_type=jnp.float32,
            precision=highest,
        )
        if update == 0:
            total_rate = base_rate + summed[:, :branches]
            summed = summed[:, branches:]
        coupled = summed.reshape(home_rows, branches, columns)
        phonon_state = (1.0 - damping) * phonon_state + damping * (
            driven + coupled
        ) / total_rate[:, :, None]
    return phonon_state.reshape(home_rows, branches * columns)


def solution(mesh):
    in_specs = (
        P(("trip", "row"), None, None),
        P(("trip", "row"), None, None),
        P(("trip", "row"), None),
        P(("trip", "row")),
        P(("trip", "row"), None),
        P(("trip", "row"), None),
        P(("trip", "row"), None),
    )
    out_specs = P(("trip", "row"), None)
    return jax.shard_map(body, mesh=mesh, in_specs=in_specs, out_specs=out_specs, check_vma=False)
```

```python
import jax
import jax.numpy as jnp
from jax import lax
from jax.experimental import pallas as pl
from jax.experimental.pallas import tpu as pltpu
from jax.sharding import PartitionSpec as P

ITERS = 2
BRANCHES = 64


damping = 0.7


def ranks_of(target):
    chain_length = target.shape[0]
    matches = target[:, None] == target[None, :]
    earlier = lax.broadcasted_iota(
        jnp.int32, (chain_length, chain_length), 1
    ) < lax.broadcasted_iota(jnp.int32, (chain_length, chain_length), 0)
    return jnp.sum((matches & earlier).astype(jnp.int32), axis=1)


def slot_onehot(places, extent):
    return lax.broadcasted_iota(jnp.int32, (extent, places.shape[0]), 0) == places[None, :]


def pack_ints(places, values, extent):
    return jnp.sum(jnp.where(slot_onehot(places, extent), values[None, :], 0), axis=1)


def pack_rows(places, values, extent):
    onehot = slot_onehot(places, extent).astype(values.dtype)
    packed = jnp.dot(
        onehot, values, preferred_element_type=jnp.float32, precision=lax.Precision.HIGHEST
    )
    return packed.astype(values.dtype)


def first_kernel(place_ref, first_ref, cubic_ref, stacked_ref):
    half = BRANCHES
    wide = 2 * BRANCHES
    turned = first_ref[0].astype(jnp.float32).T.astype(jnp.bfloat16)
    step = 1024
    for start in range(0, BRANCHES * BRANCHES, step):
        part = jnp.dot(
            turned, cubic_ref[0, :, start : start + step], preferred_element_type=jnp.float32
        ).astype(jnp.bfloat16)
        for offset in range(0, step, wide):
            row = (start + offset) // wide * half
            stacked_ref[0, row : row + half, :wide] = part[:half, offset : offset + wide]
            stacked_ref[0, row : row + half, wide:] = part[half:, offset : offset + wide]


def contract_first(cubic, row_table, row_place):
    count = cubic.shape[0]
    half = BRANCHES
    rows = half * half // 2
    return pl.pallas_call(
        first_kernel,
        grid_spec=pltpu.PrefetchScalarGridSpec(
            num_scalar_prefetch=1,
            grid=(count,),
            in_specs=[
                pl.BlockSpec((1, half, 2 * half), lambda t, place: (place[t], 0, 0)),
                pl.BlockSpec((1, half, half * half), lambda t, place: (t, 0, 0)),
            ],
            out_specs=pl.BlockSpec((1, rows, 4 * half), lambda t, place: (t, 0, 0)),
        ),
        out_shape=jax.ShapeDtypeStruct((count, rows, 4 * half), jnp.bfloat16),
        compiler_params=pltpu.CompilerParams(vmem_limit_bytes=60 * 1024 * 1024),
        cost_estimate=pl.CostEstimate(
            flops=count * 4 * half**4, bytes_accessed=count * 6 * half**3, transcendentals=0
        ),
        name="contract_first",
    )(row_place, row_table, cubic)


def rest_kernel(place_ref, weight_ref, second_ref, third_ref, stacked_ref,
                pair_one_ref, pair_two_ref, turner, spread, column_sums, loose):
    half = BRANCHES
    wide = 2 * BRANCHES
    pairs = BRANCHES // 2
    lane = lax.broadcasted_iota(jnp.int32, (1, wide), 1)
    sign = jnp.where(lane < half, -1.0, 1.0)

    @pl.when(pl.program_id(0) == 0)
    def _():
        across = lax.broadcasted_iota(jnp.int32, (4 * half, 4 * half), 0)
        along = lax.broadcasted_iota(jnp.int32, (4 * half, 4 * half), 1)
        chosen = along == (across % 16) * 16 + across // 16
        turner[...] = jnp.where(chosen, 1.0, 0.0).astype(jnp.bfloat16)

    loose[...] = second_ref[0, :half].astype(jnp.float32)
    second = jnp.concatenate(
        [loose[pl.ds(0, pairs, stride=2), :], loose[pl.ds(1, pairs, stride=2), :]], 0
    ).T
    second = jnp.concatenate([second[:half], second[half:]], 1).astype(jnp.bfloat16)
    third = third_ref[0, :half]
    swapped = (pltpu.roll(third.astype(jnp.float32), half, 1) * sign).astype(jnp.bfloat16)
    zero = jnp.zeros_like(third)

    def paired(real_rows, imag_rows):
        return jnp.concatenate(
            [
                jnp.concatenate([real_rows, zero, imag_rows, zero], 0),
                jnp.concatenate([zero, real_rows, zero, imag_rows], 0),
            ],
            1,
        )

    mixer = paired(third, swapped)
    mixer_swapped = paired(swapped, -third)
    tile = 16
    group = 8
    total = jnp.zeros((half, wide), jnp.float32)
    for first in range(0, half, tile):
        slot = first // tile % 2
        for low in range(0, pairs, tile):
            block = jnp.concatenate(
                [
                    stacked_ref[0, p * half + first : p * half + first + tile, :]
                    for p in range(low, low + tile)
                ],
                0,
            )
            block = jnp.dot(turner[...], block, preferred_element_type=jnp.float32)
            block = block.astype(jnp.bfloat16)
            plain = jnp.dot(block, mixer, preferred_element_type=jnp.float32).astype(jnp.bfloat16)
            other = jnp.dot(block, mixer_swapped, preferred_element_type=jnp.float32).astype(
                jnp.bfloat16
            )
            for side in range(2):
                value = plain[:, side * wide : (side + 1) * wide]
                turned = other[:, side * wide : (side + 1) * wide]
                row = side * pairs + low
                for a in range(tile):
                    place = slice(a * wide, (a + 1) * wide)
                    chosen = slice(a * tile, (a + 1) * tile)
                    spread[slot, row : row + tile, place] = value[chosen]
                    spread[slot, half + row : half + row + tile, place] = turned[chosen]
        for part in range(0, tile, group):
            found = jnp.dot(
                second, spread[slot, :, part * wide : (part + group) * wide],
                preferred_element_type=jnp.float32,
            )
            square = found * found
            begin = first + part
            for q in range(group):
                over = jnp.sum(square[:, q * wide : (q + 1) * wide], 1, keepdims=True)
                total = jnp.where(lane == begin + q, over, total)
            sums = jnp.sum(square, 0, keepdims=True)
            column_sums[begin : begin + group, :] = jnp.concatenate(
                [sums[:, q * wide : (q + 1) * wide] for q in range(group)], 0
            )
    weight = weight_ref[pl.program_id(0)].astype(jnp.float32)
    full = column_sums[...]
    full = (full + pltpu.roll(full, half, 1)) * weight
    pair_one_ref[0] = (total * weight).T[:half].astype(jnp.bfloat16)
    pair_two_ref[0] = full[:, :half].astype(jnp.bfloat16)


def contract_rest(stacked, far_table, far_place, weights):
    count = stacked.shape[0]
    half = BRANCHES
    wide = 2 * half
    rows = half * half // 2
    slab = far_table.shape[1]

    def block(*shape):
        return pl.BlockSpec((1,) + shape, lambda t, place, weight: (t, 0, 0))

    pair = jax.ShapeDtypeStruct((count, half, half), jnp.bfloat16)
    return pl.pallas_call(
        rest_kernel,
        grid_spec=pltpu.PrefetchScalarGridSpec(
            num_scalar_prefetch=2,
            grid=(count,),
            in_specs=[
                pl.BlockSpec((1, slab, wide), lambda t, place, weight: (place[2 * t], 0, 0)),
                pl.BlockSpec((1, slab, wide), lambda t, place, weight: (place[2 * t + 1], 0, 0)),
                block(rows, 2 * wide),
            ],
            out_specs=[block(half, half), block(half, half)],
            scratch_shapes=[
                pltpu.VMEM((2 * wide, 2 * wide), jnp.bfloat16),
                pltpu.VMEM((2, wide, 16 * wide), jnp.bfloat16),
                pltpu.VMEM((half, wide), jnp.float32),
                pltpu.VMEM((half, wide), jnp.float32),
            ],
        ),
        out_shape=[pair, pair],
        compiler_params=pltpu.CompilerParams(vmem_limit_bytes=40 * 1024 * 1024),
        name="contract_rest",
    )(far_place, weights, far_table, far_table, stacked)


def swap_kernel(in_ref, out_ref, send_sem, recv_sem, local_sem):
    count = in_ref.shape[0]
    trip = lax.axis_index("trip")
    me = lax.axis_index("row")
    barrier = pltpu.get_barrier_semaphore()
    for away in range(1, count):
        peer = lax.rem(me + away, count)
        pl.semaphore_signal(
            barrier, inc=1, device_id=(trip, peer), device_id_type=pl.DeviceIdType.MESH
        )
    pl.semaphore_wait(barrier, count - 1)
    copies = []
    for away in range(1, count):
        peer = lax.rem(me + away, count)
        copy = pltpu.make_async_remote_copy(
            src_ref=in_ref.at[peer],
            dst_ref=out_ref.at[me],
            send_sem=send_sem.at[away - 1],
            recv_sem=recv_sem.at[away - 1],
            device_id=(trip, peer),
            device_id_type=pl.DeviceIdType.MESH,
        )
        copy.start()
        copies.append(copy)
    own = pltpu.make_async_copy(in_ref.at[me], out_ref.at[me], local_sem)
    own.start()
    own.wait()
    for copy in copies:
        copy.wait()


def row_swap(value, number):
    return pl.pallas_call(
        swap_kernel,
        in_specs=[pl.BlockSpec(memory_space=pltpu.VMEM)],
        out_specs=pl.BlockSpec(memory_space=pltpu.VMEM),
        out_shape=jax.ShapeDtypeStruct(value.shape, value.dtype),
        scratch_shapes=[
            pltpu.SemaphoreType.DMA((value.shape[0] - 1,)),
            pltpu.SemaphoreType.DMA((value.shape[0] - 1,)),
            pltpu.SemaphoreType.DMA,
        ],
        compiler_params=pltpu.CompilerParams(collective_id=number, has_side_effects=True),
        cost_estimate=pl.CostEstimate(flops=0, bytes_accessed=8 * value.size, transcendentals=0),
        name="row_swap",
    )(value)


def look_up(table_rows, queries):
    looked_values = table_rows.at[queries.reshape(-1)].get(mode="promise_in_bounds")
    return looked_values.reshape(queries.shape + table_rows.shape[1:])


def exchange(value, axes):
    return lax.all_to_all(value, axes, split_axis=0, concat_axis=0, tiled=True)


def body(eigvecs, cubic, triplets, weights, deviation, source, base_rate):
    trip_count = lax.axis_size("trip")
    row_count = lax.axis_size("row")
    devices = trip_count * row_count
    everyone = ("trip", "row")
    home_rows = eigvecs.shape[0]
    branches = eigvecs.shape[1]
    trip_local = cubic.shape[0]
    columns = deviation.shape[1] // branches
    far_size = branches * columns
    slab_rows = far_size // (2 * branches)
    row_cap = trip_local // 2
    row_slots = row_count * row_cap
    home_dev = triplets[:, 0] // home_rows
    row_target = home_dev % row_count
    row_place = row_target * row_cap + ranks_of(row_target)
    row_local = triplets[:, 0] - home_dev * home_rows
    row_code = pack_ints(row_place, row_local + 1, row_slots).reshape(row_count, 1, row_cap)
    far_index = triplets[:, 1:].reshape(-1)
    far_place = far_index // home_rows
    far_queries = jnp.max(
        jnp.where(
            slot_onehot(far_place, devices), (far_index - far_place * home_rows)[None, :], 0
        ),
        axis=1,
    )
    group = lax.axis_index("trip")
    member = lax.axis_index("row")
    asked = jnp.concatenate([far_queries, row_code.reshape(-1)])
    asked = jnp.pad(asked, (0, -asked.shape[0] % 1024)).reshape(1, 8, 128)
    listed = lax.all_gather(asked, everyone, axis=0, tiled=True).reshape(devices, -1)
    queries_here = lax.dynamic_slice(
        listed, (0, group * row_count + member), (devices, 1)
    ).reshape(devices)
    arrived_codes = lax.dynamic_slice(
        listed, (group * row_count, devices + member * row_cap), (row_count, row_cap)
    )
    row_table = row_swap(look_up(eigvecs, jnp.maximum(arrived_codes - 1, 0)), 3)
    row_table = row_table.reshape((row_slots,) + eigvecs.shape[1:])
    sent = deviation.astype(jnp.bfloat16).reshape(home_rows, slab_rows, 2 * branches)
    slab = jnp.concatenate(
        [eigvecs, sent, jnp.zeros((home_rows, -slab_rows % 8, 2 * branches), jnp.bfloat16)], 1
    )
    row_table, outgoing = lax.optimization_barrier((row_table, look_up(slab, queries_here)))
    far_table = exchange(outgoing, everyone)
    stacked = contract_first(cubic, row_table, row_place)
    states = far_table[:, branches : branches + slab_rows].reshape(devices, far_size)
    states = states.at[far_place].get(mode="promise_in_bounds")
    first_pairing, second_pairing = contract_rest(stacked, far_table, far_place, weights)
    pairing = jnp.concatenate([first_pairing, second_pairing], 2)
    rates = jnp.sum(pairing.astype(jnp.float32), 2)
    highest = lax.Precision.HIGHEST
    onehot = (
        lax.broadcasted_iota(jnp.int32, (home_rows, row_slots), 0)
        == arrived_codes.reshape(-1)[None, :] - 1
    ).astype(jnp.float32)
    phonon_state = deviation.reshape(home_rows, branches, columns)
    driven = source.reshape(home_rows, branches, columns)
    for update in range(ITERS):
        if update > 0:
            outgoing = phonon_state.astype(jnp.bfloat16).reshape(sent.shape)
            states = exchange(look_up(outgoing, queries_here), everyone)
            states = states.reshape(devices, far_size)
            states = states.at[far_place].get(mode="promise_in_bounds")
        terms = jnp.einsum(
            "tab,tbc->tac",
            pairing,
            states.reshape(trip_local, 2 * branches, columns),
            preferred_element_type=jnp.float32,
        ).reshape(trip_local, branches * columns)
        if update == 0:
            terms = jnp.concatenate([rates, terms], 1)
        packed = pack_rows(row_place, terms, row_slots)
        arrived = row_swap(packed.reshape(row_count, row_cap, -1), update)
        summed = jnp.dot(
            onehot,
            arrived.reshape(row_slots, -1),
            preferred_element_type=jnp.float32,
            precision=highest,
        )
        if update == 0:
            total_rate = base_rate + summed[:, :branches]
            summed = summed[:, branches:]
        coupled = summed.reshape(home_rows, branches, columns)
        phonon_state = (1.0 - damping) * phonon_state + damping * (
            driven + coupled
        ) / total_rate[:, :, None]
    return phonon_state.reshape(home_rows, branches * columns)


def solution(mesh):
    in_specs = (
        P(("trip", "row"), None, None),
        P(("trip", "row"), None, None),
        P(("trip", "row"), None),
        P(("trip", "row")),
        P(("trip", "row"), None),
        P(("trip", "row"), None),
        P(("trip", "row"), None),
    )
    out_specs = P(("trip", "row"), None)
    return jax.shard_map(body, mesh=mesh, in_specs=in_specs, out_specs=out_specs, check_vma=False)
```
